32 devices in a mesh: dp: 8 (over y, x, core), tensor: 4 (over z).
Axes of the slice: x: 2, y: 2, z: 4, core: 2. Of those that a mesh axis runs over, the one named last changes fastest.
Arguments:
- inputs: bfloat16 [18432, 512], P(('dp', 'tensor')), may hold values from -6 to 6
- cotangent: bfloat16 [18432, 512], P(('dp', 'tensor')), may hold values from -6 to 6
- lengths: int32 [24], P('dp'), may hold values from 384 to 768, as said below
- front_norm: float32 [512], P(('dp', 'tensor')), may hold values from 0.5 to 1.5
- front_up: bfloat16 [512, 2048], P('dp', 'tensor'), may hold values from -0.25 to 0.25
- front_down: bfloat16 [2048, 512], P('tensor', 'dp'), may hold values from -0.125 to 0.125
- attend_norm: float32 [512], P(('dp', 'tensor')), may hold values from 0.5 to 1.5
- query_proj: bfloat16 [512, 512], P('dp', 'tensor'), may hold values from -0.25 to 0.25
- key_proj: bfloat16 [512, 512], P('dp', 'tensor'), may hold values from -0.25 to 0.25
- value_proj: bfloat16 [512, 512], P('dp', 'tensor'), may hold values from -0.25 to 0.25
- position_proj: bfloat16 [512, 512], P('dp', 'tensor'), may hold values from -0.25 to 0.25
- output_proj: bfloat16 [512, 512], P('tensor', 'dp'), may hold values from -1.5 to 1.5
- content_bias: float32 [512], P(('dp', 'tensor')), may hold values from -3 to 3
- position_bias: float32 [512], P(('dp', 'tensor')), may hold values from -3 to 3
- conv_norm: float32 [512], P(('dp', 'tensor')), may hold values from 0.5 to 1.5
- conv_expand: bfloat16 [512, 2, 512], P('dp', None, 'tensor'), may hold values from -0.25 to 0.25
- conv_depth: float32 [31, 512], P(None, ('dp', 'tensor')), may hold values from -1 to 1
- batch_gain: float32 [512], P(('dp', 'tensor')), may hold values from 0.5 to 1.5
- batch_shift: float32 [512], P(('dp', 'tensor')), may hold values from -3 to 3
- conv_project: bfloat16 [512, 512], P('tensor', 'dp'), may hold values from -0.25 to 0.25
- back_norm: float32 [512], P(('dp', 'tensor')), may hold values from 0.5 to 1.5
- back_up: bfloat16 [512, 2048], P('dp', 'tensor'), may hold values from -0.25 to 0.25
- back_down: bfloat16 [2048, 512], P('tensor', 'dp'), may hold values from -0.125 to 0.125
- final_norm: float32 [512], P(('dp', 'tensor')), may hold values from 0.5 to 1.5
Outputs:
- output: bfloat16 [18432, 512], P(('dp', 'tensor'))
- input_grad: bfloat16 [18432, 512], P(('dp', 'tensor'))
- front_norm_grad: float32 [512], P(('dp', 'tensor'))
- front_up_grad: float32 [512, 2048], P('dp', 'tensor')
- front_down_grad: float32 [2048, 512], P('tensor', 'dp')
- attend_norm_grad: float32 [512], P(('dp', 'tensor'))
- query_proj_grad: float32 [512, 512], P('dp', 'tensor')
- key_proj_grad: float32 [512, 512], P('dp', 'tensor')
- value_proj_grad: float32 [512, 512], P('dp', 'tensor')
- position_proj_grad: float32 [512, 512], P('dp', 'tensor')
- output_proj_grad: float32 [512, 512], P('tensor', 'dp')
- content_bias_grad: float32 [512], P(('dp', 'tensor'))
- position_bias_grad: float32 [512], P(('dp', 'tensor'))
- conv_norm_grad: float32 [512], P(('dp', 'tensor'))
- conv_expand_grad: float32 [512, 2, 512], P('dp', None, 'tensor')
- conv_depth_grad: float32 [31, 512], P(None, ('dp', 'tensor'))
- batch_gain_grad: float32 [512], P(('dp', 'tensor'))
- batch_shift_grad: float32 [512], P(('dp', 'tensor'))
- conv_project_grad: float32 [512, 512], P('tensor', 'dp')
- back_norm_grad: float32 [512], P(('dp', 'tensor'))
- back_up_grad: float32 [512, 2048], P('dp', 'tensor')
- back_down_grad: float32 [2048, 512], P('tensor', 'dp')
- final_norm_grad: float32 [512], P(('dp', 'tensor'))
The draws below stay inside these ranges and needn't reach their ends.
Inputs may be any that keep to these rules, and one draw needn't show every extreme that they name: The first lengths[s] slots of sequence s hold tokens, the rest padding; some sequence is full and some holds exactly 384 tokens.
All inputs are finite; a program needn't handle non-finite values.
Results may differ from the reference program's by a relative error of at most 0.03.
Values may be sent and summed in bfloat16 or wider, within the bound.
No kernel may reach another device: no remote copies, remote signals or barrier semaphores. Data moves between devices by JAX's collectives and lax.ppermute only.
A program may use at most 192 MiB of HBM per device.

```python
import math
import jax
import jax.numpy as jnp
from jax import lax

D = 512
HEADS = 8
FF = 2048
KERNEL = 31
SEQLEN = 768
HEAD_DIM = 64
SEQS = 24
TOKENS = 18432


def draw_lengths(key, part):
    key_base = jax.random.fold_in(key, 11)
    key_long = jax.random.fold_in(key, 12)
    key_short = jax.random.fold_in(key, 13)
    drawn = jax.random.randint(key_base, (SEQS,), SEQLEN // 2, SEQLEN + 1)
    longest = jax.random.randint(key_long, (), 0, SEQS)
    offset = jax.random.randint(key_short, (), 1, SEQS)
    shortest = (longest + offset) % SEQS
    places = jnp.arange(SEQS)
    drawn = jnp.where(places == longest, SEQLEN, drawn)
    drawn = jnp.where(places == shortest, SEQLEN // 2, drawn)
    return drawn.astype(jnp.int32)


def block_levels(rng, extent, cuts, smallest, high):
    factor_of = 1.0
    for axis_at, blocks in cuts:
        steps = jax.random.uniform(jax.random.fold_in(jax.random.fold_in(rng, 6), axis_at), (blocks,), jnp.float32, smallest / len(cuts), high / len(cuts))
        factor_of = factor_of * jnp.repeat(jnp.exp(steps), extent[axis_at] // blocks).reshape((-1,) + (1,) * (len(extent) - 1 - axis_at))
    return factor_of


def gaussian(key, extent, scale, limit, cuts=(), kind=jnp.bfloat16):
    factor_of = block_levels(key, extent, cuts, -0.22, 0.18) if cuts else 1.0
    values = jax.random.normal(key, extent, jnp.float32) * scale * factor_of
    return jnp.minimum(jnp.maximum(values, -limit), limit).astype(kind)


def setup_inputs(seed: int = 0) -> dict:
    key_of = jax.random.split(jax.random.key(seed), 25)
    return {
        "inputs": gaussian(key_of[0], (TOKENS, D), 1.0, 6.0, ((0, 32),)),
        "cotangent": gaussian(key_of[1], (TOKENS, D), 1.0, 6.0, ((0, 32),)),
        "lengths": draw_lengths(jax.random.fold_in(key_of[24], 71), 0),
        "front_norm": jnp.clip(1.0 + 0.1 * jax.random.normal(key_of[3], (D,), jnp.float32), 0.5, 1.5),
        "front_up": gaussian(key_of[4], (D, FF), D ** -0.5, 0.25, ((0, 8), (1, 4))),
        "front_down": gaussian(key_of[5], (FF, D), FF ** -0.5, 0.125, ((0, 4), (1, 8))),
        "attend_norm": jnp.clip(1.0 + 0.1 * jax.random.normal(key_of[6], (D,), jnp.float32), 0.5, 1.5),
        "query_proj": gaussian(key_of[7], (D, D), D ** -0.5, 0.25, ((0, 8), (1, 4))),
        "key_proj": gaussian(key_of[8], (D, D), D ** -0.5, 0.25, ((0, 8), (1, 4))),
        "value_proj": gaussian(key_of[9], (D, D), D ** -0.5, 0.25, ((0, 8), (1, 4))),
        "position_proj": gaussian(key_of[10], (D, D), D ** -0.5, 0.25, ((0, 8), (1, 4))),
        "output_proj": gaussian(key_of[11], (D, D), (D // 32) ** -0.5, 1.5, ((0, 4), (1, 8))),
        "content_bias": gaussian(key_of[12], (D,), 0.5, 3.0, ((0, 32),), jnp.float32),
        "position_bias": gaussian(key_of[13], (D,), 0.5, 3.0, ((0, 32),), jnp.float32),
        "conv_norm": jnp.clip(1.0 + 0.1 * jax.random.normal(key_of[14], (D,), jnp.float32), 0.5, 1.5),
        "conv_expand": gaussian(key_of[15], (D, 2, D), D ** -0.5, 0.25, ((0, 8), (2, 4))),
        "conv_depth": gaussian(key_of[16], (KERNEL, D), KERNEL ** -0.5, 1.0, ((1, 32),), jnp.float32),
        "batch_gain": jnp.clip(1.0 + 0.1 * jax.random.normal(key_of[17], (D,), jnp.float32), 0.5, 1.5),
        "batch_shift": gaussian(key_of[18], (D,), 0.5, 3.0, ((0, 32),), jnp.float32),
        "conv_project": gaussian(key_of[19], (D, D), D ** -0.5, 0.25, ((0, 4), (1, 8))),
        "back_norm": jnp.clip(1.0 + 0.1 * jax.random.normal(key_of[20], (D,), jnp.float32), 0.5, 1.5),
        "back_up": gaussian(key_of[21], (D, FF), D ** -0.5, 0.25, ((0, 8), (1, 4))),
        "back_down": gaussian(key_of[22], (FF, D), FF ** -0.5, 0.125, ((0, 4), (1, 8))),
        "final_norm": jnp.clip(1.0 + 0.1 * jax.random.normal(key_of[23], (D,), jnp.float32), 0.5, 1.5),
    }


@jax.custom_vjp
def low(v):
    return lax.optimization_barrier(v.astype(jnp.bfloat16)).astype(jnp.float32)

@jax.custom_vjp
def low_back(v):
    return v

def low_keep(v):
    return (low(v), None)

def low_pass(kept, grad):
    return (grad,)

def back_keep(v):
    return (v, None)

def back_low(kept, grad):
    return (low(grad),)
low.defvjp(low_keep, low_pass)
low_back.defvjp(back_keep, back_low)
highest = lax.Precision.HIGHEST
epsilon = 1e-05
masked_score = -1000000000.0

def matmul(left, right):
    return jnp.dot(left, right, precision=highest)

def layer_norm(values, gain):
    center = values - lax.optimization_barrier(jnp.mean(values, axis=-1, keepdims=True))
    variance = lax.optimization_barrier(jnp.mean(center * center, axis=-1, keepdims=True))
    return center * lax.rsqrt(variance + epsilon) * gain

def positions_table(length, width):
    distance = jnp.arange(2 * length - 1).astype(jnp.float32) - (length - 1)
    frequency = jnp.exp(jnp.arange(width // 2).astype(jnp.float32) * (-2.0 * math.log(10000.0) / width))
    angles = distance[:, None] * frequency[None, :]
    return jnp.stack([jnp.sin(angles), jnp.cos(angles)], axis=-1).reshape(2 * length - 1, width)

def relative_index(length):
    places = jnp.arange(length).astype(jnp.int32)
    return places[:, None] - places[None, :] + (length - 1)

def depthwise(signal, kernel):
    margin = (kernel.shape[0] - 1) // 2
    padded = jnp.pad(signal, ((0, 0), (margin, margin), (0, 0)))
    length = signal.shape[1]
    summed = jnp.zeros(signal.shape, signal.dtype)
    for offset in range(kernel.shape[0]):
        summed = summed + padded[:, offset:offset + length, :] * kernel[offset]
    return summed

def feed_forward(values, gain, weight_up, weight_down):
    normed = low(layer_norm(values, gain))
    inner = low_back(matmul(normed, weight_up))
    active = low(jax.nn.silu(inner))
    return low_back(matmul(active, weight_down))

def attend_sequence(query_content, query_position, keys, value_rows, position_rows, length):
    scale = HEAD_DIM ** (-0.5)
    content = jnp.einsum('ihe,jhe->hij', query_content, keys, precision=highest)
    lookup = jnp.einsum('ihe,rhe->hir', query_position, position_rows, precision=highest)
    index = jnp.broadcast_to(relative_index(SEQLEN)[None], content.shape)
    shifted = jnp.take_along_axis(lookup, index, axis=2)
    scores = low_back(scale * (content + shifted))
    keep = jnp.arange(SEQLEN) < length
    scores = jnp.where(keep[None, None, :], scores, masked_score)
    weights = jax.nn.softmax(scores, axis=-1)
    return jnp.einsum('hij,jhe->ihe', low(weights), value_rows, precision=highest)

def attention(values, lengths, gain, query_proj, key_proj, value_proj, position_proj, output_proj, content_bias, position_bias):
    normed = low(layer_norm(values, gain))
    query = low_back(matmul(normed, query_proj))
    keys = low_back(low(matmul(normed, key_proj)))
    value_rows = low_back(low(matmul(normed, value_proj)))
    query_content = low_back(low(query + content_bias))
    query_position = low_back(low(query + position_bias))
    position_rows = low(matmul(low(positions_table(SEQLEN, D)), position_proj)).reshape(2 * SEQLEN - 1, HEADS, HEAD_DIM)
    split_shape = (-1, SEQLEN, HEADS, HEAD_DIM)

    def one_sequence(pieces):
        return attend_sequence(pieces[0], pieces[1], pieces[2], pieces[3], position_rows, pieces[4])
    mixed = lax.map(jax.checkpoint(one_sequence), (query_content.reshape(split_shape), query_position.reshape(split_shape), keys.reshape(split_shape), value_rows.reshape(split_shape), lengths))
    mixed = low_back(low(mixed.reshape(-1, D)))
    return low_back(matmul(mixed, output_proj))

def convolution(values, valid_rows, count, gain, conv_expand, conv_depth, batch_gain, batch_shift, conv_project):
    normed = low(layer_norm(values, gain))
    expanded = low_back(matmul(normed, conv_expand.reshape(D, 2 * D)))
    gated = expanded[:, :D] * jax.nn.sigmoid(expanded[:, D:]) * valid_rows
    depth = depthwise(gated.reshape(-1, SEQLEN, D), conv_depth).reshape(-1, D)
    batch_mean = lax.optimization_barrier(jnp.sum(depth * valid_rows, axis=0)) / count
    center = depth - batch_mean
    batch_var = lax.optimization_barrier(jnp.sum(center * center * valid_rows, axis=0)) / count
    batch_hat = center * lax.rsqrt(batch_var + epsilon)
    active = low(jax.nn.silu(batch_hat * batch_gain + batch_shift))
    return low_back(matmul(active, conv_project))

def forward(lengths, inputs, front_norm, front_up, front_down, attend_norm, query_proj, key_proj, value_proj, position_proj, output_proj, content_bias, position_bias, conv_norm, conv_expand, conv_depth, batch_gain, batch_shift, conv_project, back_norm, back_up, back_down, final_norm):
    valid_rows = (jnp.arange(SEQLEN)[None, :] < lengths[:, None]).astype(jnp.float32).reshape(-1, 1)
    count = jnp.sum(lengths).astype(jnp.float32)
    first = inputs + 0.5 * feed_forward(inputs, front_norm, front_up, front_down)
    second = first + attention(first, lengths, attend_norm, query_proj, key_proj, value_proj, position_proj, output_proj, content_bias, position_bias)
    third = second + convolution(second, valid_rows, count, conv_norm, conv_expand, conv_depth, batch_gain, batch_shift, conv_project)
    fourth = third + 0.5 * feed_forward(third, back_norm, back_up, back_down)
    return layer_norm(fourth, final_norm)

def reference(inputs, cotangent, lengths, front_norm, front_up, front_down, attend_norm, query_proj, key_proj, value_proj, position_proj, output_proj, content_bias, position_bias, conv_norm, conv_expand, conv_depth, batch_gain, batch_shift, conv_project, back_norm, back_up, back_down, final_norm):
    parameters = (front_norm, front_up, front_down, attend_norm, query_proj, key_proj, value_proj, position_proj, output_proj, content_bias, position_bias, conv_norm, conv_expand, conv_depth, batch_gain, batch_shift, conv_project, back_norm, back_up, back_down, final_norm)
    floats = tuple((parameter.astype(jnp.float32) for parameter in parameters))

    def wrapped(values, *weights):
        return forward(lengths, values, *weights)
    result, pullback = jax.vjp(wrapped, inputs.astype(jnp.float32), *floats)
    grads = pullback(cotangent.astype(jnp.float32))
    return (result.astype(jnp.bfloat16), grads[0].astype(jnp.bfloat16), grads[1], grads[2], grads[3], grads[4], grads[5], grads[6], grads[7], grads[8], grads[9], grads[10], grads[11], grads[12], grads[13], grads[14], grads[15], grads[16], grads[17], grads[18], grads[19], grads[20], grads[21])
```

```python
import math

import jax
import jax.numpy as jnp
from jax import lax
from jax.experimental import pallas as pl
from jax.experimental.pallas import tpu as pltpu
from jax.sharding import PartitionSpec as P

SEQLEN = 768
HEAD_DIM = 64
BLOCK = 192
PAIR = 2 * HEAD_DIM
LOOKUP = 1024
epsilon = 1e-05
masked_score = -1000000000.0
bf = jnp.bfloat16
f32 = jnp.float32


def layer_norm(values, gain):
    center = values - jnp.mean(values, axis=-1, keepdims=True)
    variance = jnp.mean(center * center, axis=-1, keepdims=True)
    return center * lax.rsqrt(variance + epsilon) * gain


def norm_back(values, gain, upstream):
    return jax.vjp(layer_norm, values, gain)[1](upstream)


def silu_back(inner, upstream):
    return jax.vjp(jax.nn.silu, inner)[1](upstream)[0]


def dot(left, right):
    return jnp.dot(left, right, preferred_element_type=f32)


def dot_t(left, right):
    return lax.dot_general(left, right, (((1,), (1,)), ((), ())), preferred_element_type=f32)


def t_dot(left, right):
    return lax.dot_general(left, right, (((0,), (0,)), ((), ())), preferred_element_type=f32)


def reversed_table(width, rows):
    fine = 32
    lanes = jnp.arange(width)
    frequency = jnp.exp((lanes // 2).astype(f32) * (-2.0 * math.log(10000.0) / width))
    odd = (lanes % 2) == 1
    coarse_at = (SEQLEN - 1 - fine * jnp.arange(rows // fine)).astype(f32)[:, None] * frequency
    fine_at = -jnp.arange(fine).astype(f32)[:, None] * frequency
    sin_c, cos_c = jnp.sin(coarse_at), jnp.cos(coarse_at)
    first = jnp.where(odd, cos_c, sin_c)
    second = jnp.where(odd, -sin_c, cos_c)
    table = first[:, None, :] * jnp.cos(fine_at)[None] + second[:, None, :] * jnp.sin(fine_at)[None]
    return table.reshape(rows, width).astype(bf)


def bit_of(index, bit):
    return (index >> bit) & 1


def swap(value, axis, bit):
    size = lax.axis_size(axis)
    return lax.ppermute(value, axis, [(i, i ^ (1 << bit)) for i in range(size)])


def shift(value, step):
    size = lax.axis_size("tensor")
    pairs = [(i, i + step) for i in range(size) if 0 <= i + step < size]
    return lax.ppermute(value, "tensor", pairs)


def bits(axis):
    return (lax.axis_size(axis) - 1).bit_length()


def dp_orders():
    high = list(range(1, bits("dp")))
    return high + [0], high[::-1] + [0]


def pair_up(value, axis, bit, at):
    other = swap(value, axis, bit)
    mine = bit_of(lax.axis_index(axis), bit) == 0
    low = jnp.where(mine, value, other)
    high = jnp.where(mine, other, value)
    return low, high


def gather_columns(block):
    for bit in range(bits("tensor")):
        low, high = pair_up(block, "tensor", bit, 1)
        block = jnp.concatenate([low, high], axis=-1)
    return block


def gather_rows(block, order):
    done = []
    for bit in order:
        low, high = pair_up(block, "dp", bit, 0)
        place = sum(1 for d in done if d > bit)
        block = jnp.stack([low, high], axis=place)
        done.append(bit)
    return block.reshape((-1, block.shape[-1]))


def scatter_grad(grad, order):
    count = bits("dp")
    rows = grad.shape[0] >> count
    block = grad.reshape((2,) * count + (rows, grad.shape[1]))
    left = sorted(order, reverse=True)
    for bit in order[::-1]:
        place = left.index(bit)
        mine = bit_of(lax.axis_index("dp"), bit)
        keep = lax.dynamic_index_in_dim(block, mine, place, keepdims=False)
        send = lax.dynamic_index_in_dim(block, 1 - mine, place, keepdims=False)
        left.remove(bit)
        got = swap(send, "dp", bit)
        block = (keep.astype(f32) + got.astype(f32)).astype(bf)
    slices = lax.axis_size("tensor")
    width = grad.shape[1] // slices
    parts = [block[:, i * width : (i + 1) * width] for i in range(slices)]
    for bit in range(bits("tensor")):
        mine = bit_of(lax.axis_index("tensor"), bit) == 0
        low, high = parts[0::2], parts[1::2]
        keep = [jnp.where(mine, a, b) for a, b in zip(low, high)]
        send = [jnp.where(mine, b, a) for a, b in zip(low, high)]
        got = swap(jnp.concatenate(send, axis=1), "tensor", bit)
        parts = [
            k.astype(f32) + got[:, i * width : (i + 1) * width].astype(f32)
            for i, k in enumerate(keep)
        ]
        if bit + 1 < bits("tensor"):
            parts = [p.astype(bf) for p in parts]
    return parts[0]


def total_sum(value):
    for axis in ("dp", "tensor"):
        for bit in range(bits(axis)):
            value = value + swap(value, axis, bit)
    return value


def merge_stats(count, mean, spread):
    for axis in ("dp", "tensor"):
        for bit in range(bits(axis)):
            packed = jnp.concatenate([mean, spread, jnp.broadcast_to(count, mean.shape)], axis=0)
            other = swap(packed, axis, bit)
            mean_b, spread_b, count_b = other[0:1], other[1:2], other[2:3, 0:1]
            both = jnp.maximum(count + count_b, 1.0)
            delta = mean - mean_b
            spread = spread + spread_b + delta * delta * (count * count_b / both)
            mean = (count * mean + count_b * mean_b) / both
            count = count + count_b
    return count, mean, spread


def select_lanes(top, bottom):
    lanes = lax.broadcasted_iota(jnp.int32, top.shape, 1)
    return jnp.where(lanes < HEAD_DIM, top, bottom)


def stack_heads(value):
    lanes = lax.broadcasted_iota(jnp.int32, value.shape, 1)
    zero = jnp.zeros_like(value)
    return jnp.concatenate(
        [jnp.where(lanes < HEAD_DIM, value, zero), jnp.where(lanes < HEAD_DIM, zero, value)], axis=0
    )


def masked_scores(query_c, query_p, keys, rows, length):
    lookup = dot_t(query_p, rows)
    moved = [
        pltpu.roll(part, LOOKUP - (BLOCK - 1), 1, stride=1, stride_axis=0)[:, :SEQLEN]
        for part in (lookup[:BLOCK], lookup[BLOCK:])
    ]
    scores = dot_t(query_c, keys) + jnp.concatenate(moved, axis=0)
    places = lax.broadcasted_iota(jnp.int32, scores.shape, 1)
    return jnp.where(places < length, scores, masked_score)


def attend_kernel(
    key_at, row_at, lengths, window, table, wq, wk, wv, wp, bias_c, bias_p,
    mixed, log_total, keys, values, query_c, query_p, rows,
):
    block = pl.program_id(1)
    own = query_c.shape[0]

    @pl.when(block == 0)
    def _():
        query = dot(window[own : 2 * own, :], wq[...])
        scale = HEAD_DIM ** (-0.5)
        query_c[...] = (query + bias_c[...]).astype(bf) * jnp.asarray(scale, bf)
        query_p[...] = (query + bias_p[...]).astype(bf) * jnp.asarray(scale, bf)
        keys[...] = dot(window[...], wk[...]).astype(bf)
        values[...] = dot(window[...], wv[...]).astype(bf)
        rows[...] = dot(table[...], wp[...]).astype(bf)

    here = pl.ds(pl.multiple_of(block * BLOCK, BLOCK), BLOCK)
    near = pl.ds(pl.multiple_of(key_at[block], BLOCK), SEQLEN)
    span = pl.ds(pl.multiple_of(row_at[block], BLOCK), LOOKUP)
    scores = masked_scores(
        stack_heads(query_c[here, :]), stack_heads(query_p[here, :]),
        keys[near, :], rows[span, :], lengths[block],
    )
    top = jnp.max(scores, axis=1, keepdims=True)
    exponent = jnp.exp(scores - top)
    summed = jnp.sum(exponent, axis=1, keepdims=True)
    result = dot(exponent.astype(bf), values[near, :]) / summed
    mixed[...] = select_lanes(result[:BLOCK], result[BLOCK:]).astype(bf)
    total = jnp.broadcast_to(top + jnp.log(summed), result.shape)
    log_total[...] = select_lanes(total[:BLOCK], total[BLOCK:])


def attend_back_kernel(
    key_at, row_at, lengths, keys, values, query_c, query_p, rows, log_total, grad,
    content_grad, position_grad, keys_grad, values_grad, rows_grad, keys_sum, values_sum, rows_sum,
):
    block = pl.program_id(1)

    @pl.when(block == 0)
    def _():
        keys_sum[...] = jnp.zeros_like(keys_sum)
        values_sum[...] = jnp.zeros_like(values_sum)
        rows_sum[...] = jnp.zeros_like(rows_sum)

    near = pl.ds(pl.multiple_of(key_at[block], BLOCK), SEQLEN)
    span = pl.ds(pl.multiple_of(row_at[block], BLOCK), LOOKUP)
    scale = HEAD_DIM ** (-0.5)
    stacked_c = stack_heads(query_c[...])
    stacked_p = stack_heads(query_p[...])
    stacked_g = stack_heads(grad[...])
    near_keys = keys[near, :]
    near_rows = rows[span, :]
    scores = masked_scores(stacked_c, stacked_p, near_keys, near_rows, lengths[block])
    totals = jnp.concatenate([log_total[:, 0:1], log_total[:, HEAD_DIM : HEAD_DIM + 1]], axis=0)
    probs = jnp.exp(scores - totals)
    values_sum[near, :] += t_dot(probs.astype(bf), stacked_g)
    probs_grad = dot_t(stacked_g, values[near, :])
    weighted = jnp.sum(probs * probs_grad, axis=1, keepdims=True)
    scores_grad = (probs * (probs_grad - weighted)).astype(bf)
    keys_sum[near, :] += t_dot(scores_grad, stacked_c)
    content = dot(scores_grad, near_keys)
    content_grad[...] = (select_lanes(content[:BLOCK], content[BLOCK:]) * scale).astype(bf)
    turn_rows = lax.broadcasted_iota(jnp.int32, (BLOCK, BLOCK), 0)
    turn_columns = lax.broadcasted_iota(jnp.int32, (BLOCK, BLOCK), 1)
    turn = jnp.where(turn_rows + turn_columns == BLOCK - 1, 1.0, 0.0).astype(bf)
    pad = jnp.zeros((BLOCK, LOOKUP - SEQLEN), f32)
    turned = []
    for part in (scores_grad[:BLOCK], scores_grad[BLOCK:]):
        wide = jnp.concatenate([dot(turn, part), pad], axis=1)
        turned.append(pltpu.roll(wide, 0, 1, stride=1, stride_axis=0).astype(bf))
    lookup_grad = jnp.concatenate(turned, axis=0)
    position = dot(lookup_grad, near_rows)
    position = (select_lanes(position[:BLOCK], position[BLOCK:]) * scale).astype(bf)
    position_grad[...] = dot(turn, position).astype(bf)
    turned_p = stack_heads(dot(turn, query_p[...]).astype(bf))
    rows_sum[span, :] += t_dot(lookup_grad, turned_p)

    @pl.when(block == pl.num_programs(1) - 1)
    def _():
        keys_grad[...] = keys_sum[...].astype(bf)
        values_grad[...] = values_sum[...].astype(bf)
        rows_grad[...] = rows_sum[...].astype(bf)


def attend(scalars, window, table, weights, biases):
    reach, width = window.shape
    span = table.shape[0]
    own = reach // 3
    blocks = own // BLOCK
    pairs = width // PAIR
    column = lambda n: pl.BlockSpec((n, PAIR), lambda p, b, *_: (0, p))
    tile = pl.BlockSpec((BLOCK, PAIR), lambda p, b, *_: (b, p))
    whole = lambda n: pl.BlockSpec((n, width), lambda p, b, *_: (0, 0))
    return pl.pallas_call(
        attend_kernel,
        grid_spec=pltpu.PrefetchScalarGridSpec(
            num_scalar_prefetch=3,
            grid=(pairs, blocks),
            in_specs=[whole(reach), whole(span)] + [column(width)] * 4 + [column(1)] * 2,
            out_specs=[tile, tile, column(reach), column(reach), column(own), column(own), column(span)],
        ),
        out_shape=[
            jax.ShapeDtypeStruct((own, width), bf),
            jax.ShapeDtypeStruct((own, width), f32),
            jax.ShapeDtypeStruct((reach, width), bf),
            jax.ShapeDtypeStruct((reach, width), bf),
            jax.ShapeDtypeStruct((own, width), bf),
            jax.ShapeDtypeStruct((own, width), bf),
            jax.ShapeDtypeStruct((span, width), bf),
        ],
        name="attend",
    )(*scalars, window, table, *weights, *biases)


def attend_back(scalars, keys, values, query_c, query_p, rows, log_total, grad):
    reach, width = keys.shape
    span = rows.shape[0]
    own = reach // 3
    blocks = own // BLOCK
    pairs = width // PAIR
    column = lambda n: pl.BlockSpec((n, PAIR), lambda p, b, *_: (0, p))
    tile = pl.BlockSpec((BLOCK, PAIR), lambda p, b, *_: (b, p))
    return pl.pallas_call(
        attend_back_kernel,
        grid_spec=pltpu.PrefetchScalarGridSpec(
            num_scalar_prefetch=3,
            grid=(pairs, blocks),
            in_specs=[column(reach), column(reach), tile, tile, column(span), tile, tile],
            out_specs=[tile, tile, column(reach), column(reach), column(span)],
            scratch_shapes=[
                pltpu.VMEM((reach, PAIR), f32),
                pltpu.VMEM((reach, PAIR), f32),
                pltpu.VMEM((span, PAIR), f32),
            ],
        ),
        out_shape=[
            jax.ShapeDtypeStruct((own, width), bf),
            jax.ShapeDtypeStruct((own, width), bf),
            jax.ShapeDtypeStruct((reach, width), bf),
            jax.ShapeDtypeStruct((reach, width), bf),
            jax.ShapeDtypeStruct((span, width), bf),
        ],
        name="attend_back",
    )(*scalars, keys, values, query_c, query_p, rows, log_total, grad)


HALO = 16


def conv_kernel(taps, padded, out):
    total = jnp.zeros(out.shape, f32)
    for k in range(taps.shape[0]):
        total = total + padded[k + 1 : k + 1 + BLOCK, :] * taps[k : k + 1, :]
    out[...] = total


def conv_back_kernel(taps, padded, gated, grad_padded, out, taps_grad):
    count = taps.shape[0]

    @pl.when(pl.program_id(1) == 0)
    def _():
        taps_grad[...] = jnp.zeros_like(taps_grad)

    grad = grad_padded[HALO : HALO + BLOCK, :]
    total = jnp.zeros(out.shape, f32)
    for k in range(count):
        low = 2 * HALO - 1 - k
        total = total + grad_padded[low : low + BLOCK, :] * taps[k : k + 1, :]
        taps_grad[k : k + 1, :] += jnp.sum(
            grad * padded[k + 1 : k + 1 + BLOCK, :], axis=0, keepdims=True
        )
    out[...] = total


def conv_specs(width, count):
    lanes = min(width, 256)
    taps = pl.BlockSpec((count, lanes), lambda c, b: (0, c))
    wide = pl.BlockSpec((None, BLOCK + 2 * HALO, lanes), lambda c, b: (b, 0, c))
    tile = pl.BlockSpec((BLOCK, lanes), lambda c, b: (b, c))
    return width // lanes, taps, wide, tile


def depthwise(taps, padded):
    blocks, _, width = padded.shape
    chunks, tap_spec, wide, tile = conv_specs(width, taps.shape[0])
    return pl.pallas_call(
        conv_kernel,
        grid=(chunks, blocks),
        in_specs=[tap_spec, wide],
        out_specs=tile,
        out_shape=jax.ShapeDtypeStruct((blocks * BLOCK, width), f32),
        name="depthwise",
    )(taps, padded)


def depthwise_back(taps, padded, grad_padded):
    blocks, _, width = padded.shape
    chunks, tap_spec, wide, tile = conv_specs(width, taps.shape[0])

    def body(taps_ref, padded_ref, grad_ref, out, taps_grad):
        conv_back_kernel(taps_ref, padded_ref, None, grad_ref, out, taps_grad)

    return pl.pallas_call(
        body,
        grid=(chunks, blocks),
        in_specs=[tap_spec, wide, wide],
        out_specs=[tile, tap_spec],
        out_shape=[
            jax.ShapeDtypeStruct((blocks * BLOCK, width), f32),
            jax.ShapeDtypeStruct(taps.shape, f32),
        ],
        name="depthwise_back",
    )(taps, padded, grad_padded)


def shards(
    inputs, cotangent, lengths, front_norm, front_up, front_down, attend_norm, query_proj,
    key_proj, value_proj, position_proj, output_proj, content_bias, position_bias, conv_norm,
    conv_expand, conv_depth, batch_gain, batch_shift, conv_project, back_norm, back_up,
    back_down, final_norm,
):
    own, width = inputs.shape
    slices = lax.axis_size("tensor")
    local = query_proj.shape[1]
    place = lax.axis_index("tensor")
    device = lax.axis_index("dp") * slices + place
    order_a, order_b = dp_orders()
    part = front_norm.shape[0]
    taps_count = conv_depth.shape[0]

    vectors = jnp.concatenate(
        [
            jnp.stack([
                front_norm, attend_norm, content_bias, position_bias, conv_norm,
                batch_gain, batch_shift, back_norm, final_norm,
            ]),
            conv_depth,
        ],
        axis=0,
    )
    for axis in ("tensor", "dp"):
        for bit in range(bits(axis)):
            low, high = pair_up(vectors, axis, bit, 1)
            vectors = jnp.concatenate([low, high], axis=1)
    (front_gain, attend_gain, content_full, position_full, conv_gain, batch_scale, batch_offset,
     back_gain, final_gain) = [vectors[i : i + 1] for i in range(9)]
    taps = vectors[9:]

    def full_pair(first, second):
        return gather_rows(gather_columns(first), order_a), gather_rows(gather_columns(second), order_b)

    def regroup(columns, sizes):
        step = columns.shape[1] // slices
        pieces = []
        for at in range(0, step, local):
            pieces += [columns[:, t * step + at : t * step + at + local] for t in range(slices)]
        return jnp.concatenate(pieces, axis=1)

    up_front, down_front = full_pair(front_up, front_down.T)
    first_mix = gather_columns(
        jnp.concatenate([query_proj, key_proj, value_proj, position_proj], axis=1)
    )
    second_mix = gather_columns(
        jnp.concatenate(
            [output_proj.T, conv_expand[:, 0], conv_expand[:, 1], conv_project.T], axis=1
        )
    )
    attend_weights = gather_rows(regroup(first_mix, 4), order_a)
    other_weights = gather_rows(regroup(second_mix, 4), order_b)
    wq, wk, wv, wp = [attend_weights[:, i * width : (i + 1) * width] for i in range(4)]
    output_t = other_weights[:, :width]
    expand_flat = other_weights[:, width : 3 * width]
    project_t = other_weights[:, 3 * width :]
    up_back, down_back = full_pair(back_up, back_down.T)

    row_at = place * own + jnp.arange(own)
    length_row = lengths[row_at // SEQLEN]
    valid = ((row_at % SEQLEN) < length_row).astype(f32)[:, None]
    blocks = own // BLOCK
    per = SEQLEN // BLOCK
    block_at = place * blocks + jnp.arange(blocks)
    sequence = block_at // per
    scalars = (
        ((sequence * per - (place - 1) * blocks) * BLOCK).astype(jnp.int32),
        (SEQLEN - BLOCK - (block_at % per) * BLOCK).astype(jnp.int32),
        lengths[sequence].astype(jnp.int32),
    )
    is_first = ((block_at % per) == 0)[:, None, None]
    is_last = ((block_at % per) == per - 1)[:, None, None]

    def with_halo(value):
        before = shift(value[-HALO:], 1)
        after = shift(value[:HALO], -1)
        padded = jnp.concatenate([before, value, after], axis=0)
        cut = jnp.stack(
            [padded[b * BLOCK : b * BLOCK + BLOCK + 2 * HALO] for b in range(blocks)]
        )
        rows = jnp.arange(BLOCK + 2 * HALO)[None, :, None]
        drop = (is_first & (rows < HALO)) | (is_last & (rows >= BLOCK + HALO))
        return jnp.where(drop, 0.0, cut)

    def feed_forward(values, gain, weight_up, weight_down):
        normed = layer_norm(values, gain).astype(bf)
        inner = dot(normed, weight_up)
        active = jax.nn.silu(inner).astype(bf)
        return dot_t(active, weight_down), (normed, inner, active)

    def feed_back(values, gain, weight_up, weight_down, saved, upstream):
        normed, inner, active = saved
        branch = (0.5 * upstream).astype(bf)
        down_grad = t_dot(branch, active).astype(bf)
        grad_inner = silu_back(inner, dot(branch, weight_down)).astype(bf)
        up_grad = t_dot(normed, grad_inner).astype(bf)
        grad_values, grad_gain = norm_back(values, gain, dot_t(grad_inner, weight_up))
        return upstream + grad_values, grad_gain, up_grad, down_grad

    zeroth = inputs.astype(f32)
    front_out, front_saved = feed_forward(zeroth, front_gain, up_front, down_front)
    first = zeroth + 0.5 * front_out
    normed = layer_norm(first, attend_gain).astype(bf)
    window = jnp.concatenate([shift(normed, 1), normed, shift(normed, -1)], axis=0)
    span = SEQLEN - BLOCK + LOOKUP
    table = reversed_table(width, span)
    mixed, log_total, keys, values, query_c, query_p, rows = attend(
        scalars, window, table, (wq, wk, wv, wp), (content_full, position_full)
    )
    second = first + dot_t(mixed, output_t)
    conv_normed = layer_norm(second, conv_gain).astype(bf)
    expanded = dot(conv_normed, expand_flat)
    value_half, gate_half = expanded[:, :width], expanded[:, width:]
    gate = jax.nn.sigmoid(gate_half)
    gated = value_half * gate * valid
    padded = with_halo(gated)
    depth = depthwise(taps, padded)
    here_count = jnp.sum(valid, axis=0, keepdims=True)
    here_mean = jnp.sum(depth * valid, axis=0, keepdims=True) / jnp.maximum(here_count, 1.0)
    here_off = depth - here_mean
    here_spread = jnp.sum(here_off * here_off * valid, axis=0, keepdims=True)
    count, batch_mean, spread = merge_stats(here_count, here_mean, here_spread)
    inverse = lax.rsqrt(spread / count + epsilon)
    batch_hat = (depth - batch_mean) * inverse
    batch_pre = batch_hat * batch_scale + batch_offset
    conv_active = jax.nn.silu(batch_pre).astype(bf)
    third = second + dot_t(conv_active, project_t)
    back_out, back_saved = feed_forward(third, back_gain, up_back, down_back)
    fourth = third + 0.5 * back_out
    output = layer_norm(fourth, final_gain).astype(bf)

    grad_fourth, final_gain_grad = norm_back(fourth, final_gain, cotangent.astype(f32))
    grad_third, back_gain_grad, back_up_grad, back_down_grad = feed_back(
        third, back_gain, up_back, down_back, back_saved, grad_fourth
    )
    back_up_out = scatter_grad(back_up_grad, order_a)
    back_down_out = scatter_grad(back_down_grad, order_b).T
    conv_grad = grad_third.astype(bf)
    project_grad = t_dot(conv_grad, conv_active).astype(bf)
    grad_pre = silu_back(batch_pre, dot(conv_grad, project_t))
    sums = total_sum(
        jnp.concatenate(
            [
                jnp.sum(grad_pre, axis=0, keepdims=True),
                jnp.sum(grad_pre * batch_hat, axis=0, keepdims=True),
            ],
            axis=0,
        )
    )
    shift_all, gain_all = sums[0:1], sums[1:2]
    grad_depth = (
        inverse
        * batch_scale
        * (grad_pre - valid * (shift_all / count) - valid * batch_hat * (gain_all / count))
    )
    gated_grad, taps_grad = depthwise_back(taps, padded, with_halo(grad_depth))
    gated_grad = gated_grad * valid * gate
    expanded_grad = jnp.concatenate(
        [gated_grad, gated_grad * value_half * (1.0 - gate)], axis=1
    ).astype(bf)
    expand_grad = t_dot(conv_normed, expanded_grad).astype(bf)
    conv_back_values, conv_gain_grad = norm_back(second, conv_gain, dot_t(expanded_grad, expand_flat))
    grad_second = grad_third + conv_back_values
    attend_grad = grad_second.astype(bf)
    output_grad = t_dot(attend_grad, mixed).astype(bf)
    grad_mixed = dot(attend_grad, output_t).astype(bf)
    content_grad, position_grad, keys_grad, values_grad, rows_grad = attend_back(
        scalars, keys, values, query_c, query_p, rows, log_total, grad_mixed
    )
    query_grad = (content_grad.astype(f32) + position_grad.astype(f32)).astype(bf)
    content_sum = jnp.sum(content_grad, axis=0, dtype=f32, keepdims=True)
    position_sum = jnp.sum(position_grad, axis=0, dtype=f32, keepdims=True)
    attend_weight_grad = jnp.concatenate(
        [
            t_dot(normed, query_grad).astype(bf),
            t_dot(window, keys_grad).astype(bf),
            t_dot(window, values_grad).astype(bf),
            t_dot(table, rows_grad).astype(bf),
        ],
        axis=1,
    )

    def split_back(columns):
        pieces = []
        for t in range(slices):
            for at in range(0, columns.shape[1], width):
                pieces.append(columns[:, at + t * local : at + (t + 1) * local])
        return jnp.concatenate(pieces, axis=1)

    other_grad = jnp.concatenate([output_grad, expand_grad, project_grad], axis=1)
    attend_out = scatter_grad(split_back(attend_weight_grad), order_a)
    other_out = scatter_grad(split_back(other_grad), order_b)
    reach_grad = dot_t(keys_grad, wk) + dot_t(values_grad, wv)
    from_before = shift(reach_grad[2 * own :].astype(bf), 1)
    from_after = shift(reach_grad[:own].astype(bf), -1)
    normed_grad = (
        dot_t(query_grad, wq)
        + reach_grad[own : 2 * own]
        + from_before.astype(f32)
        + from_after.astype(f32)
    )
    attend_back_values, attend_gain_grad = norm_back(first, attend_gain, normed_grad)
    grad_first = grad_second + attend_back_values
    grad_zeroth, front_gain_grad, front_up_grad, front_down_grad = feed_back(
        zeroth, front_gain, up_front, down_front, front_saved, grad_first
    )
    input_grad = grad_zeroth.astype(bf)
    front_up_out = scatter_grad(front_up_grad, order_a)
    front_down_out = scatter_grad(front_down_grad, order_b).T
    small = total_sum(
        jnp.concatenate(
            [
                front_gain_grad, attend_gain_grad, content_sum, position_sum, conv_gain_grad,
                back_gain_grad, final_gain_grad, taps_grad,
            ],
            axis=0,
        )
    )
    small = lax.dynamic_slice_in_dim(
        jnp.concatenate([small, gain_all, shift_all], axis=0), device * part, part, axis=1
    )
    return (
        output,
        input_grad,
        small[0],
        front_up_out,
        front_down_out,
        small[1],
        attend_out[:, :local],
        attend_out[:, local : 2 * local],
        attend_out[:, 2 * local : 3 * local],
        attend_out[:, 3 * local :],
        other_out[:, :local].T,
        small[2],
        small[3],
        small[4],
        jnp.stack([other_out[:, local : 2 * local], other_out[:, 2 * local : 3 * local]], axis=1),
        small[7 : 7 + taps_count],
        small[7 + taps_count],
        small[8 + taps_count],
        other_out[:, 3 * local :].T,
        small[5],
        back_up_out,
        back_down_out,
        small[6],
    )


def solution(mesh):
    both = P(("dp", "tensor"))
    rows = P(("dp", "tensor"), None)
    into = P("dp", "tensor")
    out_of = P("tensor", "dp")
    halves = P("dp", None, "tensor")
    taps = P(None, ("dp", "tensor"))
    return jax.shard_map(
        shards,
        mesh=mesh,
        in_specs=(
            rows, rows, P("dp"), both, into, out_of, both, into, into, into, into, out_of,
            both, both, both, halves, taps, both, both, out_of, both, into, out_of, both,
        ),
        out_specs=(
            rows, rows, both, into, out_of, both, into, into, into, into, out_of,
            both, both, both, halves, taps, both, both, out_of, both, into, out_of, both,
        ),
        check_vma=False,
    )
```
